128 devices in a mesh: wide: 16 (over z, x), narrow: 8 (over y, core).
Axes of the slice: x: 4, y: 4, z: 4, core: 2. Of those that a mesh axis runs over, the one named last changes fastest.
Arguments:
- tokens: bfloat16 [6144, 2560], P(('wide', 'narrow')), may hold values from -6 to 6
- scores: float32 [6144], P(('wide', 'narrow')), may hold values from 0.25 to 1
- expert_ids: int32 [6144], P(('wide', 'narrow')), may hold values from 0 to 63, as said below
- gate_halves: bfloat16 [128, 2560, 2048], P(('wide', 'narrow')), may hold values from -0.125 to 0.125
- up_halves: bfloat16 [128, 2560, 2048], P(('wide', 'narrow')), may hold values from -0.125 to 0.125
- shared_gate: bfloat16 [2560, 4096], P(None, 'narrow'), may hold values from -0.125 to 0.125
- shared_up: bfloat16 [2560, 4096], P(None, 'narrow'), may hold values from -0.125 to 0.125
Outputs:
- routed_hidden: bfloat16 [6144, 4096], P(('wide', 'narrow'))
- shared_hidden: bfloat16 [6144, 4096], P('wide', 'narrow')
The draws below stay inside these ranges and needn't reach their ends.
Inputs may be any that keep to these rules, and one draw needn't show every extreme that they name: `expert_ids`: within the 48 rows of each device no expert is named more than 2 times, and one expert, the same for every device, is named exactly 2 times in the rows of every device.
All inputs are finite; a program needn't handle non-finite values.
Results may differ from the reference program's by a relative error of at most 0.0058.
Values may be sent and summed in bfloat16 or wider, within the bound.
No kernel may reach another device: no remote copies, remote signals or barrier semaphores. Data moves between devices by JAX's collectives and lax.ppermute only.
A program may use at most 128 MiB of HBM per device.

```python
import jax
import jax.numpy as jnp
from jax import lax

D = 2560
FE = 4096
FS = 4096
CAP = 2
EXPERTS = 64
ROWS_DEV = 48
TOKENS = 6144
DEVICES = 128


def draw_expert_ids(key, part):
    hot_key, rest_key = jax.random.split(jax.random.fold_in(key, 11))
    hot_expert = jax.random.randint(hot_key, (), 0, EXPERTS).astype(jnp.int32)
    block_keys = jax.random.split(rest_key, TOKENS // ROWS_DEV)

    def one_block(block_key):
        pick_key, place_key = jax.random.split(block_key)
        shuffled = jax.random.permutation(pick_key, (EXPERTS - 1) * CAP)
        others = (shuffled[:ROWS_DEV - CAP] // CAP).astype(jnp.int32)
        others = others + (others >= hot_expert).astype(jnp.int32)
        chosen = jnp.concatenate([jnp.full((CAP,), hot_expert, jnp.int32), others])
        return jax.random.permutation(place_key, chosen)
    return jax.vmap(one_block)(block_keys).reshape(TOKENS).astype(jnp.int32)


def level_of(own_key, extent, shards, least, largest):
    gain = 1.0
    for axis_at, shards_of in shards:
        steps = jax.random.uniform(jax.random.fold_in(jax.random.fold_in(own_key, 6), axis_at), (shards_of,), jnp.float32, least / len(shards), largest / len(shards))
        gain = gain * jnp.repeat(jnp.exp(steps), extent[axis_at] // shards_of).reshape((-1,) + (1,) * (len(extent) - 1 - axis_at))
    return gain


def scatter_about(own_key, dims, width, bound, cuts=(), kind=jnp.bfloat16):
    result = jax.random.normal(own_key, dims, jnp.float32) * width
    if len(cuts) > 0:
        result = level_of(own_key, dims, cuts, -0.22, 0.18) * result
    return jnp.clip(result, min=-bound, max=bound).astype(kind)


def setup_inputs(seed: int = 0) -> dict:
    streams_of = jax.random.split(jax.random.key(seed), 8)
    tokens = scatter_about(streams_of[0], (TOKENS, D), 1.0, 6.0, ((0, 128),))
    scores = jnp.clip(0.25 + 0.75 * jax.random.uniform(streams_of[1], (TOKENS,), jnp.float32) ** level_of(streams_of[1], (TOKENS,), ((0, 128),), -0.2, 0.2), 0.25, 1.0)
    expert_ids = draw_expert_ids(jax.random.fold_in(streams_of[7], 71), 0)
    gate_halves = scatter_about(streams_of[3], (2 * EXPERTS, D, FE // 2), D ** -0.5, 0.125, ((0, 128),))
    up_halves = scatter_about(streams_of[4], (2 * EXPERTS, D, FE // 2), D ** -0.5, 0.125, ((0, 128),))
    shared_gate = scatter_about(streams_of[5], (D, FS), D ** -0.5, 0.125, ((1, 8),))
    shared_up = scatter_about(streams_of[6], (D, FS), D ** -0.5, 0.125, ((1, 8),))
    return {"tokens": tokens, "scores": scores, "expert_ids": expert_ids, "gate_halves": gate_halves, "up_halves": up_halves, "shared_gate": shared_gate, "shared_up": shared_up}


def swiglu_rows(inputs, gate_matrix, up_matrix):
    gate_val = jnp.dot(inputs, gate_matrix, preferred_element_type=jnp.float32)
    up_val = jnp.dot(inputs, up_matrix, preferred_element_type=jnp.float32)
    return (jax.nn.silu(gate_val) * up_val).astype(jnp.bfloat16)


def reference(tokens, scores, expert_ids, gate_halves, up_halves, shared_gate, shared_up):
    scaled = (tokens.astype(jnp.float32) * scores[:, None]).astype(jnp.bfloat16)
    capacity = CAP * DEVICES

    def one_expert(expert):
        members = jnp.nonzero(expert_ids == expert, size=capacity, fill_value=TOKENS)[0]
        picked = jnp.take(scaled, members, axis=0, mode="clip")
        gate_full = jnp.concatenate([gate_halves[2 * expert], gate_halves[2 * expert + 1]], axis=1)
        up_full = jnp.concatenate([up_halves[2 * expert], up_halves[2 * expert + 1]], axis=1)
        return swiglu_rows(picked, gate_full, up_full), members

    hidden, members = lax.map(one_expert, jnp.arange(EXPERTS, dtype=jnp.int32))
    routed = jnp.zeros((TOKENS, FE), jnp.bfloat16)
    routed = routed.at[members.reshape(-1)].set(hidden.reshape(-1, FE), mode="drop")
    shared = swiglu_rows(tokens, shared_gate, shared_up)
    return routed, shared
```

```python
import jax
import jax.numpy as jnp
from jax import lax
from jax.experimental import pallas as pl
from jax.experimental.pallas import tpu as pltpu
from jax.sharding import Mesh, PartitionSpec as P

CAP = 2
LANES = 128
TILE = 256
STAGED = 3
F32 = jnp.float32
BF16 = jnp.bfloat16
I32 = jnp.int32


def iota(shape, dim):
    return lax.broadcasted_iota(I32, shape, dim)


def column(row, n):
    eye = iota((n, n), 0) == iota((n, n), 1)
    return jnp.sum(jnp.where(eye, jnp.broadcast_to(row, (n, n)), 0), axis=1, keepdims=True)


def dispatch_kernel(tokens_ref, scores_ref, ids_ref, send_ref):
    n, width = tokens_ref.shape
    pieces = 8 // CAP
    part = width // pieces
    ids_row = ids_ref[...].reshape(1, n)
    ids_col = column(ids_row, n)
    score_col = column(scores_ref[...].reshape(1, n), n)
    tokens = tokens_ref[...]
    scaled = (tokens.astype(F32) * score_col).astype(BF16)
    earlier = (ids_col == ids_row) & (iota((n, n), 0) < iota((n, n), 1))
    rank_row = jnp.sum(earlier.astype(I32), axis=0, keepdims=True)
    entry = 8 * ids_row + pieces * rank_row
    rows = iota((send_ref.shape[0], n), 0)
    hot = jnp.concatenate(
        [(rows == entry + j).astype(F32).astype(BF16) for j in range(pieces)], axis=1
    )
    stack = jnp.concatenate([scaled[:, j * part : (j + 1) * part] for j in range(pieces)], axis=0)
    send_ref[...] = jnp.dot(hot, stack, preferred_element_type=F32).astype(BF16)


def dispatch(tokens, scores, expert_ids, chips):
    n, width = tokens.shape
    return pl.pallas_call(
        dispatch_kernel,
        out_shape=jax.ShapeDtypeStruct((chips * 8, width * CAP // 8), BF16),
        compiler_params=pltpu.CompilerParams(vmem_limit_bytes=60 << 20),
        name="dispatch",
        cost_estimate=pl.CostEstimate(flops=10**8, bytes_accessed=2 * 10**6, transcendentals=0),
    )(tokens, scores, expert_ids)


def silu_mul(gate, up):
    return gate / (1.0 + jnp.exp(-gate)) * up


def tiles(units):
    pieces = 8 // CAP
    return [(q, j) for q in range(units // pieces // TILE) for j in range(pieces)]


def tile_of(ref, q, j):
    start = j * (ref.shape[1] * CAP // 8) + q * TILE
    return ref.at[:, start : start + TILE]


def stage_kernel(gate_ref, up_ref, gate_out, up_out, sems):
    copies = []
    for i, (q, j) in enumerate(tiles(gate_ref.shape[1])[: gate_out.shape[0]]):
        copies.append(pltpu.make_async_copy(tile_of(gate_ref, q, j), gate_out.at[i], sems.at[0, i]))
        copies.append(pltpu.make_async_copy(tile_of(up_ref, q, j), up_out.at[i], sems.at[1, i]))
    for copy in copies:
        copy.start()
    for copy in copies:
        copy.wait()


def stage(gate, up, count):
    shape = (count, gate.shape[0], TILE)
    return pl.pallas_call(
        stage_kernel,
        out_shape=(pltpu.VMEM(shape, BF16), pltpu.VMEM(shape, BF16)),
        in_specs=[pl.BlockSpec(memory_space=pltpu.HBM)] * 2,
        out_specs=(pl.BlockSpec(memory_space=pltpu.VMEM),) * 2,
        scratch_shapes=[pltpu.SemaphoreType.DMA((2, count))],
        compiler_params=pltpu.CompilerParams(vmem_limit_bytes=1 << 20),
        name="stage",
        cost_estimate=pl.CostEstimate(flops=0, bytes_accessed=10**7, transcendentals=0),
    )(gate, up)


def routed_kernel(
    own_ref, other_ref, gate_ref, up_ref, gate_first, up_first, out_ref, rows_ref, hidden_ref,
    gate_rest, up_rest, sems,
):
    core = lax.axis_index("core")
    chips = own_ref.shape[0] // 8
    part = own_ref.shape[1]
    pieces = 8 // CAP
    order = tiles(gate_ref.shape[1])
    first = gate_first.shape[0]
    copies = []
    for i, (q, j) in enumerate(order[first:]):
        copies.append(
            (
                pltpu.make_async_copy(tile_of(gate_ref, q, j), gate_rest.at[i], sems.at[0, i]),
                pltpu.make_async_copy(tile_of(up_ref, q, j), up_rest.at[i], sems.at[1, i]),
            )
        )
    for pair in copies:
        for copy in pair:
            copy.start()
    to = iota((8 * chips, 8 * chips), 0)
    at = 8 * (to % chips) + pieces * (to // chips % CAP) + to // (CAP * chips)
    perm = (iota((8 * chips, 8 * chips), 1) == at).astype(F32).astype(BF16)
    for c, ref in enumerate((own_ref, other_ref)):
        moved = jnp.dot(perm, ref[...], preferred_element_type=F32).astype(BF16)
        at = CAP * chips * c
        for j in range(pieces):
            rows_ref[at : at + CAP * chips, j * part : (j + 1) * part] = moved[
                j * CAP * chips : (j + 1) * CAP * chips
            ]
    for i, (q, j) in enumerate(order):
        if i < first:
            gate_tile, up_tile = gate_first.at[i], up_first.at[i]
        else:
            gate_tile, up_tile = gate_rest.at[i - first], up_rest.at[i - first]
            for copy in copies[i - first]:
                copy.wait()
        gate = jnp.dot(rows_ref[...], gate_tile[...], preferred_element_type=F32)
        up = jnp.dot(rows_ref[...], up_tile[...], preferred_element_type=F32)
        hidden = silu_mul(gate, up)
        for c in range(2):
            core_of = core if c == 0 else 1 - core
            for s in range(CAP):
                at = chips * (CAP * c + s)
                for k in range(TILE // LANES):
                    hidden_ref[k, pl.ds(8 * core_of + pieces * s + j, chips, stride=16), :] = (
                        hidden[at : at + chips, k * LANES : (k + 1) * LANES]
                    )
        if j == pieces - 1:
            for k in range(TILE // LANES):
                lane = q * TILE + k * LANES
                out_ref[:, lane : lane + LANES] = hidden_ref[k].astype(BF16)


def routed(own, other, gate, up, gate_first, up_first):
    rows, part = own.shape
    width, units = gate.shape
    pieces = 8 // CAP
    chips = rows // 8
    rest = units // TILE - gate_first.shape[0]
    vmem = pl.BlockSpec(memory_space=pltpu.VMEM)
    hbm = pl.BlockSpec(memory_space=pltpu.HBM)
    return pl.pallas_call(
        routed_kernel,
        out_shape=jax.ShapeDtypeStruct((16 * chips, units // pieces), BF16),
        in_specs=[vmem, vmem, hbm, hbm, vmem, vmem],
        out_specs=vmem,
        scratch_shapes=[
            pltpu.VMEM((4 * chips, width), BF16),
            pltpu.VMEM((TILE // LANES, 16 * chips, LANES), F32),
            pltpu.VMEM((rest, width, TILE), BF16),
            pltpu.VMEM((rest, width, TILE), BF16),
            pltpu.SemaphoreType.DMA((2, rest)),
        ],
        compiler_params=pltpu.CompilerParams(vmem_limit_bytes=36 << 20),
        name="routed",
        cost_estimate=pl.CostEstimate(
            flops=4 * 4 * chips * width * units, bytes_accessed=10**6, transcendentals=0
        ),
    )(own, other, gate, up, gate_first, up_first)


def shared_kernel(*refs):
    gate_ref, up_ref, out_ref = refs[-3:]
    blocks = refs[:-3]
    core = lax.axis_index("core")
    y = lax.axis_index("y")
    ring = len(blocks) // 2
    n = blocks[0].shape[0]
    for c in range(2):
        rows = jnp.concatenate([ref[...] for ref in blocks[ring * c : ring * (c + 1)]], axis=0)
        gate = jnp.dot(rows, gate_ref[...], preferred_element_type=F32)
        up = jnp.dot(rows, up_ref[...], preferred_element_type=F32)
        hidden = silu_mul(gate, up).astype(BF16)
        core_of = core if c == 0 else 1 - core
        step = 1 - 2 * core_of
        for i, back in enumerate((0, 1, -1, 2)):
            from_y = lax.rem(y - back * step + 2 * ring, ring)
            at = pl.multiple_of(n * (2 * from_y + core_of), 16)
            out_ref[pl.ds(at, n), :] = hidden[n * i : n * (i + 1)]


def shared(blocks, shared_gate, shared_up):
    n, width = blocks[0].shape
    units = shared_gate.shape[1]
    tile = 256
    whole = pl.BlockSpec((n, width), lambda q: (0, 0))
    weight = pl.BlockSpec((width, tile), lambda q: (0, q))
    return pl.pallas_call(
        shared_kernel,
        out_shape=jax.ShapeDtypeStruct((len(blocks) * n, units), BF16),
        grid=(units // tile,),
        in_specs=[whole] * len(blocks) + [weight, weight],
        out_specs=pl.BlockSpec((len(blocks) * n, tile), lambda q: (0, q)),
        compiler_params=pltpu.CompilerParams(vmem_limit_bytes=32 << 20),
        name="shared",
        cost_estimate=pl.CostEstimate(
            flops=4 * len(blocks) * n * width * units, bytes_accessed=8 * 10**6, transcendentals=0
        ),
    )(*blocks, shared_gate, shared_up)


def collect_kernel(back_ref, ids_ref, out_ref):
    n = out_ref.shape[0]
    pieces = 8 // CAP
    part = back_ref.shape[1]
    ids_row = ids_ref[...].reshape(1, n)
    ids_col = column(ids_row, n)
    earlier = (ids_col == ids_row) & (iota((n, n), 1) < iota((n, n), 0))
    rank_col = jnp.sum(earlier.astype(I32), axis=1, keepdims=True)
    entry = 16 * ids_col + pieces * rank_col
    cells = iota((n, back_ref.shape[0]), 1)
    hot = jnp.concatenate(
        [
            (cells == entry + (8 * h + j)).astype(F32).astype(BF16)
            for h in range(2)
            for j in range(pieces)
        ],
        axis=0,
    )
    picked = jnp.dot(hot, back_ref[...], preferred_element_type=F32).astype(BF16)
    for q in range(2 * pieces):
        out_ref[:, q * part : (q + 1) * part] = picked[q * n : (q + 1) * n]


def collect(back, expert_ids):
    rows, part = back.shape
    n = expert_ids.shape[0]
    return pl.pallas_call(
        collect_kernel,
        out_shape=jax.ShapeDtypeStruct((n, 8 * part), BF16),
        compiler_params=pltpu.CompilerParams(vmem_limit_bytes=8 << 20),
        name="collect",
        cost_estimate=pl.CostEstimate(flops=4 * 10**8, bytes_accessed=15 * 10**5, transcendentals=0),
    )(back, expert_ids)


def swap(x):
    return lax.ppermute(x, "core", [(0, 1), (1, 0)])


def turn(x, ring, step):
    pairs = [
        (2 * y + c, 2 * ((y + step * (1 - 2 * c)) % ring) + c) for y in range(ring) for c in range(2)
    ]
    return lax.ppermute(x, ("y", "core"), pairs)


def shards(tokens, scores, expert_ids, gate_halves, up_halves, shared_gate, shared_up):
    ring = lax.axis_size("y")
    chips = lax.axis_size("wide") * ring
    send = dispatch(tokens, scores, expert_ids, chips)
    arrived = lax.all_to_all(
        send.reshape(chips, 8, send.shape[1]), ("wide", "y"), split_axis=0, concat_axis=0, tiled=True
    ).reshape(send.shape)
    after = turn(tokens, ring, 1)
    gate = pltpu.with_memory_space_constraint(gate_halves[0], pltpu.HBM)
    up = pltpu.with_memory_space_constraint(up_halves[0], pltpu.HBM)
    arrived, after, gate, up = lax.optimization_barrier((arrived, after, gate, up))
    before = turn(tokens, ring, -1)
    opposite = turn(after, ring, 1)
    arrived_other = swap(arrived)
    gate_first, up_first = stage(gate, up, STAGED)
    hidden = routed(arrived, arrived_other, gate, up, gate_first, up_first)
    hidden, before, opposite = lax.optimization_barrier((hidden, before, opposite))
    back = lax.all_to_all(
        hidden.reshape(2 * chips, 8, hidden.shape[1]),
        ("wide", "y", "core"),
        split_axis=0,
        concat_axis=0,
        tiled=True,
    ).reshape(hidden.shape)
    blocks = [tokens, after, before, opposite]
    blocks = blocks + [swap(block) for block in blocks]
    blocks = lax.optimization_barrier((*blocks, hidden))[:-1]
    shared_hidden = shared(blocks, shared_gate, shared_up)
    back, shared_hidden = lax.optimization_barrier((back, shared_hidden))
    return collect(back, expert_ids), shared_hidden


def solution(mesh):
    wide, narrow = mesh.devices.shape
    fine = Mesh(mesh.devices.reshape(wide, narrow // 2, 2), ("wide", "y", "core"))
    every = ("wide", "y", "core")
    placed = (
        P(every, None),
        P(every),
        P(every),
        P(every, None, None),
        P(every, None, None),
        P(None, ("y", "core")),
        P(None, ("y", "core")),
    )
    return jax.shard_map(
        shards,
        mesh=fine,
        in_specs=placed,
        out_specs=(P(every, None), P("wide", ("y", "core"))),
        check_vma=False,
    )
```

```python
import jax
import jax.numpy as jnp
from jax import lax
from jax.experimental import pallas as pl
from jax.experimental.pallas import tpu as pltpu
from jax.sharding import Mesh, PartitionSpec as P

CAP = 2
LANES = 128
TILE = 256
F32 = jnp.float32
BF16 = jnp.bfloat16
I32 = jnp.int32


def iota(shape, dim):
    return lax.broadcasted_iota(I32, shape, dim)


def column(row, n):
    eye = iota((n, n), 0) == iota((n, n), 1)
    return jnp.sum(jnp.where(eye, jnp.broadcast_to(row, (n, n)), 0), axis=1, keepdims=True)


def dispatch_kernel(tokens_ref, scores_ref, ids_ref, send_ref):
    n, width = tokens_ref.shape
    pieces = 8 // CAP
    part = width // pieces
    ids_row = ids_ref[...].reshape(1, n)
    ids_col = column(ids_row, n)
    score_col = column(scores_ref[...].reshape(1, n), n)
    tokens = tokens_ref[...]
    scaled = (tokens.astype(F32) * score_col).astype(BF16)
    earlier = (ids_col == ids_row) & (iota((n, n), 0) < iota((n, n), 1))
    rank_row = jnp.sum(earlier.astype(I32), axis=0, keepdims=True)
    entry = 8 * ids_row + pieces * rank_row
    rows = iota((send_ref.shape[0], n), 0)
    hot = jnp.concatenate(
        [(rows == entry + j).astype(F32).astype(BF16) for j in range(pieces)], axis=1
    )
    stack = jnp.concatenate([scaled[:, j * part : (j + 1) * part] for j in range(pieces)], axis=0)
    send_ref[...] = jnp.dot(hot, stack, preferred_element_type=F32).astype(BF16)


def dispatch(tokens, scores, expert_ids, chips):
    n, width = tokens.shape
    return pl.pallas_call(
        dispatch_kernel,
        out_shape=jax.ShapeDtypeStruct((chips * 8, width * CAP // 8), BF16),
        compiler_params=pltpu.CompilerParams(vmem_limit_bytes=8 << 20),
        name="dispatch",
        cost_estimate=pl.CostEstimate(flops=2 * 10**10, bytes_accessed=2 * 10**6, transcendentals=0),
    )(
        tokens,
        pltpu.with_memory_space_constraint(scores, pltpu.HBM),
        pltpu.with_memory_space_constraint(expert_ids, pltpu.HBM),
    )


def silu_mul(gate, up):
    return gate / (1.0 + jnp.exp(-gate)) * up


def routed_rows(rows_ref, hidden_ref, moved, gate_ref, up_ref, emit):
    chips = moved.shape[0] // 8
    part = moved.shape[1]
    pieces = 8 // CAP
    to = iota((8 * chips, 8 * chips), 0)
    at = 8 * (to % chips) + pieces * (to // chips % CAP) + to // (CAP * chips)
    perm = (iota((8 * chips, 8 * chips), 1) == at).astype(F32).astype(BF16)
    moved = jnp.dot(perm, moved, preferred_element_type=F32).astype(BF16)
    for j in range(pieces):
        rows_ref[:, j * part : (j + 1) * part] = moved[
            j * CAP * chips : (j + 1) * CAP * chips
        ]
    units = gate_ref.shape[1] // pieces
    for q in range(units // TILE):
        for j in range(pieces):
            lane = j * units + q * TILE
            gate_tile = gate_ref[:, lane : lane + TILE]
            up_tile = up_ref[:, lane : lane + TILE]
            gate = jnp.dot(rows_ref[...], gate_tile, preferred_element_type=F32)
            up = jnp.dot(rows_ref[...], up_tile, preferred_element_type=F32)
            hidden = silu_mul(gate, up)
            for s in range(CAP):
                for k in range(TILE // LANES):
                    hidden_ref[k, pl.ds(pieces * s + j, chips, stride=8), :] = hidden[
                        s * chips : (s + 1) * chips, k * LANES : (k + 1) * LANES
                    ]
        for k in range(TILE // LANES):
            emit(q, k, hidden_ref[k].reshape(chips, 8, LANES).astype(BF16))


def routed_own_kernel(own_ref, gate_ref, up_ref, out_ref, rows_ref, hidden_ref):
    def emit(q, k, block):
        lane = q * TILE + k * LANES
        out_ref[:, :, lane : lane + LANES] = block

    routed_rows(rows_ref, hidden_ref, own_ref[...], gate_ref, up_ref, emit)


def routed_other_kernel(
    other_ref, mine_ref, gate_ref, up_ref, out_ref, rows_ref, hidden_ref, block_ref, sems
):
    core = lax.axis_index("core")
    splits = block_ref.shape[2] // TILE
    first = pltpu.make_async_copy(mine_ref, out_ref.at[:, core], sems.at[splits])
    first.start()
    copies = []

    def emit(q, k, block):
        lane = q * TILE + k * LANES
        block_ref[:, :, lane : lane + LANES] = block
        if k == TILE // LANES - 1:
            lanes = slice(q * TILE, (q + 1) * TILE)
            copies.append(
                pltpu.make_async_copy(
                    block_ref.at[:, :, lanes], out_ref.at[:, 1 - core, :, lanes], sems.at[q]
                )
            )
            copies[-1].start()

    routed_rows(rows_ref, hidden_ref, other_ref[...], gate_ref, up_ref, emit)
    first.wait()
    for copy in copies:
        copy.wait()


def routed_estimate(rows, width, units):
    return pl.CostEstimate(flops=4 * rows * width * units, bytes_accessed=10**6, transcendentals=0)


def routed(own, other, gate, up):
    rows, part = own.shape
    width, units = gate.shape
    pieces = 8 // CAP
    chips = rows // 8
    vmem = pl.BlockSpec(memory_space=pltpu.VMEM)
    hbm = pl.BlockSpec(memory_space=pltpu.HBM)
    work = [
        pltpu.VMEM((CAP * chips, width), BF16),
        pltpu.VMEM((TILE // LANES, 8 * chips, LANES), F32),
    ]
    block = (chips, 8, units // pieces)
    mine = pl.pallas_call(
        routed_own_kernel,
        out_shape=pltpu.VMEM(block, BF16),
        in_specs=[vmem] * 3,
        out_specs=vmem,
        scratch_shapes=work,
        compiler_params=pltpu.CompilerParams(vmem_limit_bytes=12 << 20),
        name="routed_own",
        cost_estimate=routed_estimate(CAP * chips, width, units),
    )(own, gate, up)
    return pl.pallas_call(
        routed_other_kernel,
        out_shape=jax.ShapeDtypeStruct((chips, 2) + block[1:], BF16),
        in_specs=[vmem] * 4,
        out_specs=hbm,
        scratch_shapes=work
        + [pltpu.VMEM(block, BF16), pltpu.SemaphoreType.DMA((units // pieces // TILE + 1,))],
        compiler_params=pltpu.CompilerParams(vmem_limit_bytes=12 << 20),
        name="routed_other",
        cost_estimate=routed_estimate(CAP * chips, width, units),
    )(other, mine, gate, up)


def shared_kernel(*refs):
    gate_ref, up_ref, out_ref = refs[-3:]
    blocks = refs[:-3]
    core = lax.axis_index("core")
    y = lax.axis_index("y")
    ring = len(blocks) // 2
    n = blocks[0].shape[0]
    for c in range(2):
        rows = jnp.concatenate([ref[...] for ref in blocks[ring * c : ring * (c + 1)]], axis=0)
        gate = jnp.dot(rows, gate_ref[...], preferred_element_type=F32)
        up = jnp.dot(rows, up_ref[...], preferred_element_type=F32)
        hidden = silu_mul(gate, up).astype(BF16)
        core_of = core if c == 0 else 1 - core
        step = 1 - 2 * core_of
        for i, back in enumerate((0, 1, -1, 2)):
            from_y = lax.rem(y - back * step + 2 * ring, ring)
            at = pl.multiple_of(n * (2 * from_y + core_of), 16)
            out_ref[pl.ds(at, n), :] = hidden[n * i : n * (i + 1)]


def shared(blocks, shared_gate, shared_up):
    n, width = blocks[0].shape
    units = shared_gate.shape[1]
    tile = 256
    whole = pl.BlockSpec((n, width), lambda q: (0, 0))
    weight = pl.BlockSpec((width, tile), lambda q: (0, q))
    return pl.pallas_call(
        shared_kernel,
        out_shape=jax.ShapeDtypeStruct((len(blocks) * n, units), BF16),
        grid=(units // tile,),
        in_specs=[whole] * len(blocks) + [weight, weight],
        out_specs=pl.BlockSpec((len(blocks) * n, tile), lambda q: (0, q)),
        compiler_params=pltpu.CompilerParams(vmem_limit_bytes=32 << 20),
        name="shared",
        cost_estimate=pl.CostEstimate(
            flops=7 * 10**9, bytes_accessed=8 * 10**6, transcendentals=0
        ),
    )(*blocks, shared_gate, shared_up)


def collect_kernel(back_ref, ids_ref, out_ref):
    n = out_ref.shape[0]
    pieces = 8 // CAP
    part = back_ref.shape[1]
    ids_row = ids_ref[...].reshape(1, n)
    ids_col = column(ids_row, n)
    earlier = (ids_col == ids_row) & (iota((n, n), 1) < iota((n, n), 0))
    rank_col = jnp.sum(earlier.astype(I32), axis=1, keepdims=True)
    entry = 16 * ids_col + pieces * rank_col
    cells = iota((n, back_ref.shape[0]), 1)
    hot = jnp.concatenate(
        [
            (cells == entry + (8 * h + j)).astype(F32).astype(BF16)
            for h in range(2)
            for j in range(pieces)
        ],
        axis=0,
    )
    picked = jnp.dot(hot, back_ref[...], preferred_element_type=F32).astype(BF16)
    for q in range(2 * pieces):
        out_ref[:, q * part : (q + 1) * part] = picked[q * n : (q + 1) * n]


def collect(back, expert_ids):
    rows, part = back.shape
    n = expert_ids.shape[0]
    return pl.pallas_call(
        collect_kernel,
        out_shape=jax.ShapeDtypeStruct((n, 8 * part), BF16),
        compiler_params=pltpu.CompilerParams(vmem_limit_bytes=8 << 20),
        name="collect",
        cost_estimate=pl.CostEstimate(flops=4 * 10**8, bytes_accessed=15 * 10**5, transcendentals=0),
    )(back, expert_ids)


def swap(x):
    return lax.ppermute(x, "core", [(0, 1), (1, 0)])


def turn(x, ring, step):
    pairs = [
        (2 * y + c, 2 * ((y + step * (1 - 2 * c)) % ring) + c) for y in range(ring) for c in range(2)
    ]
    return lax.ppermute(x, ("y", "core"), pairs)


def shards(tokens, scores, expert_ids, gate_halves, up_halves, shared_gate, shared_up):
    ring = lax.axis_size("y")
    chips = lax.axis_size("wide") * ring
    send = dispatch(tokens, scores, expert_ids, chips)
    arrived = lax.all_to_all(
        send.reshape(chips, 8, send.shape[1]), ("wide", "y"), split_axis=0, concat_axis=0, tiled=True
    ).reshape(send.shape)
    gate = pltpu.with_memory_space_constraint(gate_halves[0], pltpu.VMEM)
    up = pltpu.with_memory_space_constraint(up_halves[0], pltpu.VMEM)
    arrived, mine = lax.optimization_barrier((arrived, tokens))
    arrived_other = swap(arrived)
    after = turn(mine, ring, 1)
    before = turn(mine, ring, -1)
    opposite = turn(mine, ring, 2)
    hidden = routed(arrived, arrived_other, gate, up)
    back = lax.all_to_all(
        hidden.reshape(2 * chips, 8, hidden.shape[3]),
        ("wide", "y", "core"),
        split_axis=0,
        concat_axis=0,
        tiled=True,
    ).reshape(16 * chips, hidden.shape[3])
    blocks = [tokens, after, before, opposite]
    blocks = blocks + [swap(block) for block in blocks]
    blocks = lax.optimization_barrier((*blocks, hidden))[:-1]
    shared_hidden = shared(blocks, shared_gate, shared_up)
    back, shared_hidden = lax.optimization_barrier((back, shared_hidden))
    return collect(back, expert_ids), shared_hidden


def solution(mesh):
    wide, narrow = mesh.devices.shape
    fine = Mesh(mesh.devices.reshape(wide, narrow // 2, 2), ("wide", "y", "core"))
    every = ("wide", "y", "core")
    placed = (
        P(every, None),
        P(every),
        P(every),
        P(every, None, None),
        P(every, None, None),
        P(None, ("y", "core")),
        P(None, ("y", "core")),
    )
    return jax.shard_map(
        shards,
        mesh=fine,
        in_specs=placed,
        out_specs=(P(every, None), P("wide", ("y", "core"))),
        check_vma=False,
    )
```

```python
import jax
import jax.numpy as jnp
from jax import lax
from jax.experimental import pallas as pl
from jax.experimental.pallas import tpu as pltpu
from jax.sharding import Mesh, PartitionSpec as P

CAP = 2
LANES = 128
TILE = 256
F32 = jnp.float32
BF16 = jnp.bfloat16
I32 = jnp.int32


def iota(shape, dim):
    return lax.broadcasted_iota(I32, shape, dim)


def column(row, n):
    eye = iota((n, n), 0) == iota((n, n), 1)
    return jnp.sum(jnp.where(eye, jnp.broadcast_to(row, (n, n)), 0), axis=1, keepdims=True)


def dispatch_kernel(tokens_ref, scores_ref, ids_ref, send_ref):
    n, width = tokens_ref.shape
    pieces = 8 // CAP
    part = width // pieces
    ids_row = ids_ref[...].reshape(1, n)
    ids_col = column(ids_row, n)
    score_col = column(scores_ref[...].reshape(1, n), n)
    tokens = tokens_ref[...]
    scaled = (tokens.astype(F32) * score_col).astype(BF16)
    earlier = (ids_col == ids_row) & (iota((n, n), 0) < iota((n, n), 1))
    rank_row = jnp.sum(earlier.astype(I32), axis=0, keepdims=True)
    entry = 8 * ids_row + pieces * rank_row
    rows = iota((send_ref.shape[0], n), 0)
    hot = jnp.concatenate(
        [(rows == entry + j).astype(F32).astype(BF16) for j in range(pieces)], axis=1
    )
    stack = jnp.concatenate([scaled[:, j * part : (j + 1) * part] for j in range(pieces)], axis=0)
    send_ref[...] = jnp.dot(hot, stack, preferred_element_type=F32).astype(BF16)


def dispatch(tokens, scores, expert_ids, chips):
    n, width = tokens.shape
    return pl.pallas_call(
        dispatch_kernel,
        out_shape=jax.ShapeDtypeStruct((chips * 8, width * CAP // 8), BF16),
        compiler_params=pltpu.CompilerParams(vmem_limit_bytes=8 << 20),
        name="dispatch",
        cost_estimate=pl.CostEstimate(flops=2 * 10**10, bytes_accessed=2 * 10**6, transcendentals=0),
    )(
        pltpu.with_memory_space_constraint(tokens, pltpu.HBM),
        pltpu.with_memory_space_constraint(scores, pltpu.HBM),
        pltpu.with_memory_space_constraint(expert_ids, pltpu.HBM),
    )


def silu_mul(gate, up):
    return gate / (1.0 + jnp.exp(-gate)) * up


def routed_rows(rows_ref, hidden_ref, arrived_ref, gate_ref, up_ref, emit):
    chips = arrived_ref.shape[0] // 8
    part = arrived_ref.shape[1]
    pieces = 8 // CAP
    some = min(chips, 32)
    to = iota((8 * some, 1), 0)
    at = 8 * (to % some) + pieces * (to // some % CAP) + to // (CAP * some)
    perm = (iota((8 * some, 8 * some), 1) == at).astype(F32).astype(BF16)
    for g in range(chips // some):
        block = jnp.dot(
            perm, arrived_ref[8 * some * g : 8 * some * (g + 1), :], preferred_element_type=F32
        ).astype(BF16)
        for s in range(CAP):
            to_row = chips * s + some * g
            for j in range(pieces):
                from_row = some * (CAP * j + s)
                rows_ref[to_row : to_row + some, j * part : (j + 1) * part] = block[
                    from_row : from_row + some
                ]
    units = gate_ref.shape[1] // pieces
    for q in range(units // TILE):
        for j in range(pieces):
            lane = j * units + q * TILE
            gate_tile = gate_ref[:, lane : lane + TILE]
            up_tile = up_ref[:, lane : lane + TILE]
            gate = jnp.dot(rows_ref[...], gate_tile, preferred_element_type=F32)
            up = jnp.dot(rows_ref[...], up_tile, preferred_element_type=F32)
            hidden = silu_mul(gate, up)
            for s in range(CAP):
                for k in range(TILE // LANES):
                    hidden_ref[k, pl.ds(pieces * s + j, chips, stride=8), :] = hidden[
                        s * chips : (s + 1) * chips, k * LANES : (k + 1) * LANES
                    ]
        for k in range(TILE // LANES):
            emit(q, k, hidden_ref[k].reshape(chips, 8, LANES).astype(BF16))


def routed_own_kernel(
    own_ref, gate_ref, up_ref, tokens_ref, partner_ref, out_ref, pair_ref, rows_ref, hidden_ref, sems
):
    copies = [
        pltpu.make_async_copy(ref, pair_ref.at[i], sems.at[i])
        for i, ref in enumerate((tokens_ref, partner_ref))
    ]
    for copy in copies:
        copy.start()

    def emit(q, k, block):
        lane = q * TILE + k * LANES
        out_ref[:, :, lane : lane + LANES] = block

    routed_rows(rows_ref, hidden_ref, own_ref, gate_ref, up_ref, emit)
    for copy in copies:
        copy.wait()


def routed_other_kernel(
    other_ref, mine_ref, gate_ref, up_ref, out_ref, rows_ref, hidden_ref, block_ref, sems
):
    core = lax.axis_index("core")
    splits = block_ref.shape[2] // TILE
    first = pltpu.make_async_copy(mine_ref, out_ref.at[:, core], sems.at[splits])
    first.start()
    copies = []

    def emit(q, k, block):
        lane = q * TILE + k * LANES
        block_ref[:, :, lane : lane + LANES] = block
        if k == TILE // LANES - 1:
            lanes = slice(q * TILE, (q + 1) * TILE)
            copies.append(
                pltpu.make_async_copy(
                    block_ref.at[:, :, lanes], out_ref.at[:, 1 - core, :, lanes], sems.at[q]
                )
            )
            copies[-1].start()

    routed_rows(rows_ref, hidden_ref, other_ref, gate_ref, up_ref, emit)
    first.wait()
    for copy in copies:
        copy.wait()


def routed_work(chips, width):
    return [
        pltpu.VMEM((CAP * chips, width), BF16),
        pltpu.VMEM((TILE // LANES, 8 * chips, LANES), F32),
    ]


def routed_estimate(rows, width, units):
    return pl.CostEstimate(flops=4 * rows * width * units, bytes_accessed=10**6, transcendentals=0)


def routed_own(own, gate, up, tokens, partner):
    rows, part = own.shape
    width, units = gate.shape
    chips = rows // 8
    vmem = pl.BlockSpec(memory_space=pltpu.VMEM)
    hbm = pl.BlockSpec(memory_space=pltpu.HBM)
    return pl.pallas_call(
        routed_own_kernel,
        out_shape=(
            pltpu.VMEM((chips, 8, units * CAP // 8), BF16),
            jax.ShapeDtypeStruct((2,) + tokens.shape, BF16),
        ),
        in_specs=[vmem] * 3 + [hbm] * 2,
        out_specs=(vmem, hbm),
        scratch_shapes=routed_work(chips, width) + [pltpu.SemaphoreType.DMA((2,))],
        compiler_params=pltpu.CompilerParams(vmem_limit_bytes=12 << 20),
        name="routed_own",
        cost_estimate=routed_estimate(CAP * chips, width, units),
    )(own, gate, up, tokens, partner)


def routed_other(other, mine, gate, up):
    width, units = gate.shape
    chips = mine.shape[0]
    vmem = pl.BlockSpec(memory_space=pltpu.VMEM)
    hbm = pl.BlockSpec(memory_space=pltpu.HBM)
    return pl.pallas_call(
        routed_other_kernel,
        out_shape=jax.ShapeDtypeStruct((chips, 2) + mine.shape[1:], BF16),
        in_specs=[vmem] * 4,
        out_specs=hbm,
        scratch_shapes=routed_work(chips, width)
        + [pltpu.VMEM(mine.shape, BF16), pltpu.SemaphoreType.DMA((mine.shape[2] // TILE + 1,))],
        compiler_params=pltpu.CompilerParams(vmem_limit_bytes=12 << 20),
        name="routed_other",
        cost_estimate=routed_estimate(CAP * chips, width, units),
    )(other, mine, gate, up)


def shared_kernel(*refs):
    gate_ref, up_ref, out_ref = refs[-3:]
    blocks = refs[:-3]
    core = lax.axis_index("core")
    y = lax.axis_index("y")
    step = 1 - 2 * core
    n = blocks[0].shape[0]
    ring = out_ref.shape[0] // (2 * n)
    places = [
        [(0, 0), (0, 1), (-1, 0), (-1, 1)],
        [(1, 1), (1, 0), (2, 0), (2, 1)],
    ]
    for group, place in ((blocks[:3], places[0]), (blocks[3:], places[1])):
        rows = jnp.concatenate(
            [ref[...].reshape(-1, ref.shape[-1]) for ref in group], axis=0
        )
        gate = jnp.dot(rows, gate_ref[...], preferred_element_type=F32)
        up = jnp.dot(rows, up_ref[...], preferred_element_type=F32)
        hidden = silu_mul(gate, up).astype(BF16)
        for i, (ahead, flip) in enumerate(place):
            from_y = lax.rem(y + ahead * step + 2 * ring, ring)
            from_core = 1 - core if flip else core
            at = pl.multiple_of(n * (2 * from_y + from_core), 16)
            out_ref[pl.ds(at, n), :] = hidden[n * i : n * (i + 1)]


def whole_block(x):
    return pl.BlockSpec(x.shape, lambda q: (0,) * x.ndim)


def shared(blocks, shared_gate, shared_up, rows):
    width, units = shared_gate.shape
    tile = 256
    weight = pl.BlockSpec((width, tile), lambda q: (0, q))
    return pl.pallas_call(
        shared_kernel,
        out_shape=jax.ShapeDtypeStruct((rows, units), BF16),
        grid=(units // tile,),
        in_specs=[whole_block(block) for block in blocks] + [weight, weight],
        out_specs=pl.BlockSpec((rows, tile), lambda q: (0, q)),
        compiler_params=pltpu.CompilerParams(vmem_limit_bytes=32 << 20),
        name="shared",
        cost_estimate=pl.CostEstimate(flops=5 * 10**9, bytes_accessed=8 * 10**6, transcendentals=0),
    )(*blocks, shared_gate, shared_up)


def collect_kernel(back_ref, ids_ref, out_ref):
    n = out_ref.shape[0]
    pieces = 8 // CAP
    part = back_ref.shape[1]
    ids_row = ids_ref[...].reshape(1, n)
    ids_col = column(ids_row, n)
    earlier = (ids_col == ids_row) & (iota((n, n), 1) < iota((n, n), 0))
    rank_col = jnp.sum(earlier.astype(I32), axis=1, keepdims=True)
    entry = 16 * ids_col + pieces * rank_col
    cells = iota((n, back_ref.shape[0]), 1)
    hot = jnp.concatenate(
        [
            (cells == entry + (8 * h + j)).astype(F32).astype(BF16)
            for h in range(2)
            for j in range(pieces)
        ],
        axis=0,
    )
    picked = jnp.dot(hot, back_ref[...], preferred_element_type=F32).astype(BF16)
    for q in range(2 * pieces):
        out_ref[:, q * part : (q + 1) * part] = picked[q * n : (q + 1) * n]


def collect(back, expert_ids):
    rows, part = back.shape
    n = expert_ids.shape[0]
    return pl.pallas_call(
        collect_kernel,
        out_shape=jax.ShapeDtypeStruct((n, 8 * part), BF16),
        compiler_params=pltpu.CompilerParams(vmem_limit_bytes=8 << 20),
        name="collect",
        cost_estimate=pl.CostEstimate(flops=4 * 10**8, bytes_accessed=15 * 10**5, transcendentals=0),
    )(back, expert_ids)


def swap(x):
    return lax.ppermute(x, "core", [(0, 1), (1, 0)])


def turn(x, ring):
    pairs = [(2 * y + c, 2 * ((y + 1 - 2 * c) % ring) + c) for y in range(ring) for c in range(2)]
    return lax.ppermute(x, ("y", "core"), pairs)


def shards(tokens, scores, expert_ids, gate_halves, up_halves, shared_gate, shared_up):
    ring = lax.axis_size("y")
    chips = lax.axis_size("wide") * ring
    partner = swap(tokens)
    send = dispatch(tokens, scores, expert_ids, chips)
    send, partner = lax.optimization_barrier((send, partner))
    arrived = lax.all_to_all(
        send.reshape(chips, 8, send.shape[1]), ("wide", "y"), split_axis=0, concat_axis=0, tiled=True
    ).reshape(send.shape)
    gate = pltpu.with_memory_space_constraint(gate_halves[0], pltpu.VMEM)
    up = pltpu.with_memory_space_constraint(up_halves[0], pltpu.VMEM)
    arrived, mine = lax.optimization_barrier((arrived, tokens))
    arrived_other = swap(arrived)
    opposite = lax.ppermute(mine, "y", [(y, (y + ring // 2) % ring) for y in range(ring)])
    own_hidden, pair = routed_own(arrived, gate, up, mine, partner)
    turned = turn(pair, ring)
    hidden = routed_other(arrived_other, own_hidden, gate, up)
    back = lax.all_to_all(
        hidden.reshape(2 * chips, 8, hidden.shape[3]),
        ("wide", "y", "core"),
        split_axis=0,
        concat_axis=0,
        tiled=True,
    ).reshape(16 * chips, hidden.shape[3])
    turned, opposite, _ = lax.optimization_barrier((turned, opposite, hidden))
    blocks = (tokens, partner, turned, swap(turned), opposite, swap(opposite))
    shared_hidden = shared(blocks, shared_gate, shared_up, 2 * ring * tokens.shape[0])
    back, shared_hidden = lax.optimization_barrier((back, shared_hidden))
    return collect(back, expert_ids), shared_hidden


def solution(mesh):
    wide, narrow = mesh.devices.shape
    fine = Mesh(mesh.devices.reshape(wide, narrow // 2, 2), ("wide", "y", "core"))
    every = ("wide", "y", "core")
    placed = (
        P(every, None),
        P(every),
        P(every),
        P(every, None, None),
        P(every, None, None),
        P(None, ("y", "core")),
        P(None, ("y", "core")),
    )
    return jax.shard_map(
        shards,
        mesh=fine,
        in_specs=placed,
        out_specs=(P(every, None), P("wide", ("y", "core"))),
        check_vma=False,
    )
```

```python
import jax
import jax.numpy as jnp
from jax import lax
from jax.experimental import pallas as pl
from jax.experimental.pallas import tpu as pltpu
from jax.sharding import Mesh, PartitionSpec as P

CAP = 2
LANES = 128
TILE = 256
F32 = jnp.float32
BF16 = jnp.bfloat16
I32 = jnp.int32


def iota(shape, dim):
    return lax.broadcasted_iota(I32, shape, dim)


def column(row, n):
    eye = iota((n, n), 0) == iota((n, n), 1)
    return jnp.sum(jnp.where(eye, jnp.broadcast_to(row, (n, n)), 0), axis=1, keepdims=True)


def dispatch_kernel(tokens_ref, scores_ref, ids_ref, send_ref):
    n, width = tokens_ref.shape
    pieces = 8 // CAP
    part = width // pieces
    ids_row = ids_ref[...].reshape(1, n)
    ids_col = column(ids_row, n)
    score_col = column(scores_ref[...].reshape(1, n), n)
    tokens = tokens_ref[...]
    scaled = (tokens.astype(F32) * score_col).astype(BF16)
    earlier = (ids_col == ids_row) & (iota((n, n), 0) < iota((n, n), 1))
    rank_row = jnp.sum(earlier.astype(I32), axis=0, keepdims=True)
    entry = 8 * ids_row + pieces * rank_row
    entries = jnp.concatenate([entry + j for j in range(pieces)], axis=1)
    hot = (iota((send_ref.shape[0], pieces * n), 0) == entries).astype(F32).astype(BF16)
    stack = jnp.concatenate([scaled[:, j * part : (j + 1) * part] for j in range(pieces)], axis=0)
    send_ref[...] = jnp.dot(hot, stack, preferred_element_type=F32).astype(BF16)


def dispatch(tokens, scores, expert_ids, chips):
    n, width = tokens.shape
    return pl.pallas_call(
        dispatch_kernel,
        out_shape=jax.ShapeDtypeStruct((chips * 8, width * CAP // 8), BF16),
        compiler_params=pltpu.CompilerParams(vmem_limit_bytes=8 << 20),
        name="dispatch",
        cost_estimate=pl.CostEstimate(flops=2 * 10**10, bytes_accessed=2 * 10**6, transcendentals=0),
    )(
        pltpu.with_memory_space_constraint(tokens, pltpu.HBM),
        pltpu.with_memory_space_constraint(scores, pltpu.HBM),
        pltpu.with_memory_space_constraint(expert_ids, pltpu.HBM),
    )


def silu_mul(gate, up):
    return gate / (1.0 + jnp.exp(-gate)) * up


def routed_rows(rows_ref, hidden_ref, arrived_ref, gate_ref, up_ref, emit):
    chips = arrived_ref.shape[0] // 8
    part = arrived_ref.shape[1]
    pieces = 8 // CAP
    some = min(chips, 32)
    to = iota((8 * some, 1), 0)
    at = 8 * (to % some) + pieces * (to // some % CAP) + to // (CAP * some)
    perm = (iota((8 * some, 8 * some), 1) == at).astype(F32).astype(BF16)
    for g in range(chips // some):
        block = jnp.dot(
            perm, arrived_ref[8 * some * g : 8 * some * (g + 1), :], preferred_element_type=F32
        ).astype(BF16)
        for s in range(CAP):
            to_row = chips * s + some * g
            for j in range(pieces):
                from_row = some * (CAP * j + s)
                rows_ref[to_row : to_row + some, j * part : (j + 1) * part] = block[
                    from_row : from_row + some
                ]
    units = gate_ref.shape[1] // pieces
    for q in range(units // TILE):
        for j in range(pieces):
            lane = j * units + q * TILE
            gate_tile = gate_ref[:, lane : lane + TILE]
            up_tile = up_ref[:, lane : lane + TILE]
            gate = jnp.dot(rows_ref[...], gate_tile, preferred_element_type=F32)
            up = jnp.dot(rows_ref[...], up_tile, preferred_element_type=F32)
            hidden = silu_mul(gate, up)
            for s in range(CAP):
                for k in range(TILE // LANES):
                    hidden_ref[k, pl.ds(pieces * s + j, chips, stride=8), :] = hidden[
                        s * chips : (s + 1) * chips, k * LANES : (k + 1) * LANES
                    ]
        for k in range(TILE // LANES):
            emit(q, k, hidden_ref[k].reshape(chips, 8, LANES).astype(BF16))


def routed_own_kernel(
    own_ref, gate_ref, up_ref, tokens_ref, partner_ref, out_ref, pair_ref, rows_ref, hidden_ref, sems
):
    copies = [
        pltpu.make_async_copy(ref, pair_ref.at[i], sems.at[i])
        for i, ref in enumerate((tokens_ref, partner_ref))
    ]
    for copy in copies:
        copy.start()

    def emit(q, k, block):
        lane = q * TILE + k * LANES
        out_ref[:, :, lane : lane + LANES] = block

    routed_rows(rows_ref, hidden_ref, own_ref, gate_ref, up_ref, emit)
    for copy in copies:
        copy.wait()


def routed_other_kernel(
    other_ref, mine_ref, gate_ref, up_ref, out_ref, rows_ref, hidden_ref, block_ref, sems
):
    core = lax.axis_index("core")
    splits = block_ref.shape[2] // TILE
    first = pltpu.make_async_copy(mine_ref, out_ref.at[:, core], sems.at[splits])
    first.start()
    copies = []

    def emit(q, k, block):
        lane = q * TILE + k * LANES
        block_ref[:, :, lane : lane + LANES] = block
        if k == TILE // LANES - 1:
            lanes = slice(q * TILE, (q + 1) * TILE)
            copies.append(
                pltpu.make_async_copy(
                    block_ref.at[:, :, lanes], out_ref.at[:, 1 - core, :, lanes], sems.at[q]
                )
            )
            copies[-1].start()

    routed_rows(rows_ref, hidden_ref, other_ref, gate_ref, up_ref, emit)
    first.wait()
    for copy in copies:
        copy.wait()


def routed_work(chips, width):
    return [
        pltpu.VMEM((CAP * chips, width), BF16),
        pltpu.VMEM((TILE // LANES, 8 * chips, LANES), F32),
    ]


def routed_estimate(rows, width, units):
    return pl.CostEstimate(flops=4 * rows * width * units, bytes_accessed=10**6, transcendentals=0)


def routed_own(own, gate, up, tokens, partner):
    rows, part = own.shape
    width, units = gate.shape
    chips = rows // 8
    vmem = pl.BlockSpec(memory_space=pltpu.VMEM)
    hbm = pl.BlockSpec(memory_space=pltpu.HBM)
    return pl.pallas_call(
        routed_own_kernel,
        out_shape=(
            pltpu.VMEM((chips, 8, units * CAP // 8), BF16),
            pltpu.HBM((2,) + tokens.shape, BF16),
        ),
        in_specs=[vmem] * 3 + [hbm] * 2,
        out_specs=(vmem, hbm),
        scratch_shapes=routed_work(chips, width) + [pltpu.SemaphoreType.DMA((2,))],
        compiler_params=pltpu.CompilerParams(vmem_limit_bytes=12 << 20),
        name="routed_own",
        cost_estimate=routed_estimate(CAP * chips, width, units),
    )(own, gate, up, tokens, partner)


def routed_other(other, mine, gate, up):
    width, units = gate.shape
    chips = mine.shape[0]
    vmem = pl.BlockSpec(memory_space=pltpu.VMEM)
    hbm = pl.BlockSpec(memory_space=pltpu.HBM)
    return pl.pallas_call(
        routed_other_kernel,
        out_shape=jax.ShapeDtypeStruct((chips, 2) + mine.shape[1:], BF16),
        in_specs=[vmem] * 4,
        out_specs=hbm,
        scratch_shapes=routed_work(chips, width)
        + [pltpu.VMEM(mine.shape, BF16), pltpu.SemaphoreType.DMA((mine.shape[2] // TILE + 1,))],
        compiler_params=pltpu.CompilerParams(vmem_limit_bytes=12 << 20),
        name="routed_other",
        cost_estimate=routed_estimate(CAP * chips, width, units),
    )(other, mine, gate, up)


def shared_kernel(*refs):
    gate_ref, up_ref, out_ref = refs[-3:]
    blocks = refs[:-3]
    core = lax.axis_index("core")
    y = lax.axis_index("y")
    step = 1 - 2 * core
    n = blocks[0].shape[0]
    ring = out_ref.shape[0] // (2 * n)
    places = [
        [(0, 0), (0, 1), (-1, 0), (-1, 1)],
        [(1, 1), (1, 0), (2, 0), (2, 1)],
    ]
    for group, place in ((blocks[:3], places[0]), (blocks[3:], places[1])):
        rows = jnp.concatenate(
            [ref[...].reshape(-1, ref.shape[-1]) for ref in group], axis=0
        )
        gate = jnp.dot(rows, gate_ref[...], preferred_element_type=F32)
        up = jnp.dot(rows, up_ref[...], preferred_element_type=F32)
        hidden = silu_mul(gate, up).astype(BF16)
        for i, (ahead, flip) in enumerate(place):
            from_y = lax.rem(y + ahead * step + 2 * ring, ring)
            from_core = 1 - core if flip else core
            at = pl.multiple_of(n * (2 * from_y + from_core), 16)
            out_ref[pl.ds(at, n), :] = hidden[n * i : n * (i + 1)]


def whole_block(x):
    return pl.BlockSpec(x.shape, lambda q: (0,) * x.ndim)


def shared(blocks, shared_gate, shared_up, rows):
    width, units = shared_gate.shape
    tile = 256
    weight = pl.BlockSpec((width, tile), lambda q: (0, q))
    return pl.pallas_call(
        shared_kernel,
        out_shape=jax.ShapeDtypeStruct((rows, units), BF16),
        grid=(units // tile,),
        in_specs=[whole_block(block) for block in blocks] + [weight, weight],
        out_specs=pl.BlockSpec((rows, tile), lambda q: (0, q)),
        compiler_params=pltpu.CompilerParams(vmem_limit_bytes=32 << 20),
        name="shared",
        cost_estimate=pl.CostEstimate(flops=5 * 10**9, bytes_accessed=8 * 10**6, transcendentals=0),
    )(
        *blocks,
        pltpu.with_memory_space_constraint(shared_gate, pltpu.HBM),
        pltpu.with_memory_space_constraint(shared_up, pltpu.HBM),
    )


def collect_kernel(back_ref, ids_ref, out_ref):
    n = out_ref.shape[0]
    pieces = 8 // CAP
    part = back_ref.shape[1]
    ids_row = ids_ref[...].reshape(1, n)
    ids_col = column(ids_row, n)
    earlier = (ids_col == ids_row) & (iota((n, n), 1) < iota((n, n), 0))
    rank_col = jnp.sum(earlier.astype(I32), axis=1, keepdims=True)
    entry = 16 * ids_col + pieces * rank_col
    cells = iota((n, back_ref.shape[0]), 1)
    hot = jnp.concatenate(
        [
            (cells == entry + (8 * h + j)).astype(F32).astype(BF16)
            for h in range(2)
            for j in range(pieces)
        ],
        axis=0,
    )
    picked = jnp.dot(hot, back_ref[...], preferred_element_type=F32).astype(BF16)
    for q in range(2 * pieces):
        out_ref[:, q * part : (q + 1) * part] = picked[q * n : (q + 1) * n]


def collect(back, expert_ids):
    rows, part = back.shape
    n = expert_ids.shape[0]
    return pl.pallas_call(
        collect_kernel,
        out_shape=jax.ShapeDtypeStruct((n, 8 * part), BF16),
        compiler_params=pltpu.CompilerParams(vmem_limit_bytes=8 << 20),
        name="collect",
        cost_estimate=pl.CostEstimate(flops=4 * 10**8, bytes_accessed=15 * 10**5, transcendentals=0),
    )(back, expert_ids)


def swap(x):
    return lax.ppermute(x, "core", [(0, 1), (1, 0)])


def turn(x, ring):
    pairs = [(2 * y + c, 2 * ((y + 1 - 2 * c) % ring) + c) for y in range(ring) for c in range(2)]
    return lax.ppermute(x, ("y", "core"), pairs)


def shards(tokens, scores, expert_ids, gate_halves, up_halves, shared_gate, shared_up):
    ring = lax.axis_size("y")
    chips = lax.axis_size("wide") * ring
    partner = swap(tokens)
    send = dispatch(tokens, scores, expert_ids, chips)
    send, partner = lax.optimization_barrier((send, partner))
    arrived = lax.all_to_all(
        send.reshape(chips, 8, send.shape[1]), ("wide", "y"), split_axis=0, concat_axis=0, tiled=True
    ).reshape(send.shape)
    gate = pltpu.with_memory_space_constraint(gate_halves[0], pltpu.VMEM)
    up = pltpu.with_memory_space_constraint(up_halves[0], pltpu.VMEM)
    arrived, mine = lax.optimization_barrier((arrived, tokens))
    arrived_other = swap(arrived)
    opposite = lax.ppermute(mine, "y", [(y, (y + ring // 2) % ring) for y in range(ring)])
    own_hidden, pair = routed_own(arrived, gate, up, mine, partner)
    turned = turn(pair, ring)
    hidden = routed_other(arrived_other, own_hidden, gate, up)
    back = lax.all_to_all(
        hidden.reshape(2 * chips, 8, hidden.shape[3]),
        ("wide", "y", "core"),
        split_axis=0,
        concat_axis=0,
        tiled=True,
    ).reshape(16 * chips, hidden.shape[3])
    turned, opposite, _ = lax.optimization_barrier((turned, opposite, hidden))
    blocks = (tokens, partner, turned, swap(turned), opposite, swap(opposite))
    shared_hidden = shared(blocks, shared_gate, shared_up, 2 * ring * tokens.shape[0])
    back, shared_hidden = lax.optimization_barrier((back, shared_hidden))
    return collect(back, expert_ids), shared_hidden


def solution(mesh):
    wide, narrow = mesh.devices.shape
    fine = Mesh(mesh.devices.reshape(wide, narrow // 2, 2), ("wide", "y", "core"))
    every = ("wide", "y", "core")
    placed = (
        P(every, None),
        P(every),
        P(every),
        P(every, None, None),
        P(every, None, None),
        P(None, ("y", "core")),
        P(None, ("y", "core")),
    )
    return jax.shard_map(
        shards,
        mesh=fine,
        in_specs=placed,
        out_specs=(P(every, None), P("wide", ("y", "core"))),
        check_vma=False,
    )
```

```python
import jax
import jax.numpy as jnp
from jax import lax
from jax.experimental import pallas as pl
from jax.experimental.pallas import tpu as pltpu
from jax.sharding import Mesh, PartitionSpec as P

CAP = 2
LANES = 128
TILE = 512
F32 = jnp.float32
BF16 = jnp.bfloat16
I32 = jnp.int32


def iota(shape, dim):
    return lax.broadcasted_iota(I32, shape, dim)


def column(row, n):
    eye = iota((n, n), 0) == iota((n, n), 1)
    return jnp.sum(jnp.where(eye, jnp.broadcast_to(row, (n, n)), 0), axis=1, keepdims=True)


def dispatch_kernel(tokens_ref, scores_ref, ids_ref, send_ref):
    n, width = tokens_ref.shape
    pieces = 8 // CAP
    part = width // pieces
    ids_row = ids_ref[...].reshape(1, n)
    ids_col = column(ids_row, n)
    score_col = column(scores_ref[...].reshape(1, n), n)
    tokens = tokens_ref[...]
    scaled = (tokens.astype(F32) * score_col).astype(BF16)
    earlier = (ids_col == ids_row) & (iota((n, n), 0) < iota((n, n), 1))
    rank_row = jnp.sum(earlier.astype(I32), axis=0, keepdims=True)
    entry = 8 * ids_row + pieces * rank_row
    entries = jnp.concatenate([entry + j for j in range(pieces)], axis=1)
    hot = (iota((send_ref.shape[0], pieces * n), 0) == entries).astype(F32).astype(BF16)
    stack = jnp.concatenate([scaled[:, j * part : (j + 1) * part] for j in range(pieces)], axis=0)
    send_ref[...] = jnp.dot(hot, stack, preferred_element_type=F32).astype(BF16)


def dispatch(tokens, scores, expert_ids, chips):
    n, width = tokens.shape
    return pl.pallas_call(
        dispatch_kernel,
        out_shape=jax.ShapeDtypeStruct((chips * 8, width * CAP // 8), BF16),
        compiler_params=pltpu.CompilerParams(vmem_limit_bytes=8 << 20),
        name="dispatch",
        cost_estimate=pl.CostEstimate(flops=2 * 10**10, bytes_accessed=2 * 10**6, transcendentals=0),
    )(
        pltpu.with_memory_space_constraint(tokens, pltpu.HBM),
        pltpu.with_memory_space_constraint(scores, pltpu.HBM),
        pltpu.with_memory_space_constraint(expert_ids, pltpu.HBM),
    )


def silu_mul(gate, up):
    return gate / (1.0 + jnp.exp(-gate)) * up


def routed_rows(rows_ref, hidden_ref, arrived_ref, gate_ref, up_ref, emit):
    chips = arrived_ref.shape[0] // 8
    part = arrived_ref.shape[1]
    pieces = 8 // CAP
    some = min(chips, 32)
    to = iota((8 * some, 1), 0)
    at = 8 * (to % some) + pieces * (to // some % CAP) + to // (CAP * some)
    perm = (iota((8 * some, 8 * some), 1) == at).astype(F32).astype(BF16)
    for g in range(chips // some):
        block = jnp.dot(
            perm, arrived_ref[8 * some * g : 8 * some * (g + 1), :], preferred_element_type=F32
        ).astype(BF16)
        for s in range(CAP):
            to_row = chips * s + some * g
            for j in range(pieces):
                from_row = some * (CAP * j + s)
                rows_ref[to_row : to_row + some, j * part : (j + 1) * part] = block[
                    from_row : from_row + some
                ]
    units = gate_ref.shape[1] // pieces
    for q in range(units // TILE):
        for j in range(pieces):
            lane = j * units + q * TILE
            gate_tile = gate_ref[:, lane : lane + TILE]
            up_tile = up_ref[:, lane : lane + TILE]
            gate = jnp.dot(rows_ref[...], gate_tile, preferred_element_type=F32)
            up = jnp.dot(rows_ref[...], up_tile, preferred_element_type=F32)
            hidden = silu_mul(gate, up)
            for s in range(CAP):
                for k in range(TILE // LANES):
                    hidden_ref[k, pl.ds(pieces * s + j, chips, stride=8), :] = hidden[
                        s * chips : (s + 1) * chips, k * LANES : (k + 1) * LANES
                    ]
        for k in range(TILE // LANES):
            emit(q, k, hidden_ref[k].reshape(chips, 8, LANES).astype(BF16))


def routed_own_kernel(
    own_ref, gate_ref, up_ref, tokens_ref, partner_ref, out_ref, pair_ref, rows_ref, hidden_ref, sems
):
    copies = [
        pltpu.make_async_copy(ref, pair_ref.at[i], sems.at[i])
        for i, ref in enumerate((tokens_ref, partner_ref))
    ]
    for copy in copies:
        copy.start()

    def emit(q, k, block):
        lane = q * TILE + k * LANES
        out_ref[:, :, lane : lane + LANES] = block

    routed_rows(rows_ref, hidden_ref, own_ref, gate_ref, up_ref, emit)
    for copy in copies:
        copy.wait()


def routed_other_kernel(
    other_ref, mine_ref, gate_ref, up_ref, out_ref, rows_ref, hidden_ref, block_ref, sems
):
    core = lax.axis_index("core")
    splits = block_ref.shape[2] // TILE
    first = pltpu.make_async_copy(mine_ref, out_ref.at[:, core], sems.at[splits])
    first.start()
    copies = []

    def emit(q, k, block):
        lane = q * TILE + k * LANES
        block_ref[:, :, lane : lane + LANES] = block
        if k == TILE // LANES - 1:
            lanes = slice(q * TILE, (q + 1) * TILE)
            copies.append(
                pltpu.make_async_copy(
                    block_ref.at[:, :, lanes], out_ref.at[:, 1 - core, :, lanes], sems.at[q]
                )
            )
            copies[-1].start()

    routed_rows(rows_ref, hidden_ref, other_ref, gate_ref, up_ref, emit)
    first.wait()
    for copy in copies:
        copy.wait()


def routed_work(chips, width):
    return [
        pltpu.VMEM((CAP * chips, width), BF16),
        pltpu.VMEM((TILE // LANES, 8 * chips, LANES), F32),
    ]


def routed_estimate(rows, width, units):
    return pl.CostEstimate(flops=4 * rows * width * units, bytes_accessed=10**6, transcendentals=0)


def routed_own(own, gate, up, tokens, partner):
    rows, part = own.shape
    width, units = gate.shape
    chips = rows // 8
    vmem = pl.BlockSpec(memory_space=pltpu.VMEM)
    hbm = pl.BlockSpec(memory_space=pltpu.HBM)
    return pl.pallas_call(
        routed_own_kernel,
        out_shape=(
            pltpu.VMEM((chips, 8, units * CAP // 8), BF16),
            pltpu.HBM((2,) + tokens.shape, BF16),
        ),
        in_specs=[vmem] * 3 + [hbm] * 2,
        out_specs=(vmem, hbm),
        scratch_shapes=routed_work(chips, width) + [pltpu.SemaphoreType.DMA((2,))],
        compiler_params=pltpu.CompilerParams(vmem_limit_bytes=12 << 20),
        name="routed_own",
        cost_estimate=routed_estimate(CAP * chips, width, units),
    )(own, gate, up, tokens, partner)


def routed_other(other, mine, gate, up):
    width, units = gate.shape
    chips = mine.shape[0]
    vmem = pl.BlockSpec(memory_space=pltpu.VMEM)
    hbm = pl.BlockSpec(memory_space=pltpu.HBM)
    return pl.pallas_call(
        routed_other_kernel,
        out_shape=jax.ShapeDtypeStruct((chips, 2) + mine.shape[1:], BF16),
        in_specs=[vmem] * 4,
        out_specs=hbm,
        scratch_shapes=routed_work(chips, width)
        + [pltpu.VMEM(mine.shape, BF16), pltpu.SemaphoreType.DMA((mine.shape[2] // TILE + 1,))],
        compiler_params=pltpu.CompilerParams(vmem_limit_bytes=12 << 20),
        name="routed_other",
        cost_estimate=routed_estimate(CAP * chips, width, units),
    )(other, mine, gate, up)


def shared_kernel(*refs):
    gate_ref, up_ref, out_ref = refs[-3:]
    blocks = refs[:-3]
    core = lax.axis_index("core")
    y = lax.axis_index("y")
    step = 1 - 2 * core
    n = blocks[0].shape[0]
    ring = out_ref.shape[0] // (2 * n)
    places = [
        [(0, 0), (0, 1), (-1, 0), (-1, 1)],
        [(1, 1), (1, 0), (2, 0), (2, 1)],
    ]
    for group, place in ((blocks[:3], places[0]), (blocks[3:], places[1])):
        rows = jnp.concatenate(
            [ref[...].reshape(-1, ref.shape[-1]) for ref in group], axis=0
        )
        gate = jnp.dot(rows, gate_ref[...], preferred_element_type=F32)
        up = jnp.dot(rows, up_ref[...], preferred_element_type=F32)
        hidden = silu_mul(gate, up).astype(BF16)
        for i, (ahead, flip) in enumerate(place):
            from_y = lax.rem(y + ahead * step + 2 * ring, ring)
            from_core = 1 - core if flip else core
            at = pl.multiple_of(n * (2 * from_y + from_core), 16)
            out_ref[pl.ds(at, n), :] = hidden[n * i : n * (i + 1)]


def whole_block(x):
    return pl.BlockSpec(x.shape, lambda q: (0,) * x.ndim)


def shared(blocks, shared_gate, shared_up, rows):
    width, units = shared_gate.shape
    tile = 256
    weight = pl.BlockSpec((width, tile), lambda q: (0, q))
    return pl.pallas_call(
        shared_kernel,
        out_shape=jax.ShapeDtypeStruct((rows, units), BF16),
        grid=(units // tile,),
        in_specs=[whole_block(block) for block in blocks] + [weight, weight],
        out_specs=pl.BlockSpec((rows, tile), lambda q: (0, q)),
        compiler_params=pltpu.CompilerParams(vmem_limit_bytes=32 << 20),
        name="shared",
        cost_estimate=pl.CostEstimate(flops=5 * 10**9, bytes_accessed=8 * 10**6, transcendentals=0),
    )(
        *blocks,
        pltpu.with_memory_space_constraint(shared_gate, pltpu.HBM),
        pltpu.with_memory_space_constraint(shared_up, pltpu.HBM),
    )


def collect_kernel(back_ref, ids_ref, out_ref):
    n = out_ref.shape[0]
    pieces = 8 // CAP
    part = back_ref.shape[1]
    ids_row = ids_ref[...].reshape(1, n)
    ids_col = column(ids_row, n)
    earlier = (ids_col == ids_row) & (iota((n, n), 1) < iota((n, n), 0))
    rank_col = jnp.sum(earlier.astype(I32), axis=1, keepdims=True)
    entry = 16 * ids_col + pieces * rank_col
    cells = iota((n, back_ref.shape[0]), 1)
    hot = jnp.concatenate(
        [
            (cells == entry + (8 * h + j)).astype(F32).astype(BF16)
            for h in range(2)
            for j in range(pieces)
        ],
        axis=0,
    )
    picked = jnp.dot(hot, back_ref[...], preferred_element_type=F32).astype(BF16)
    for q in range(2 * pieces):
        out_ref[:, q * part : (q + 1) * part] = picked[q * n : (q + 1) * n]


def collect(back, expert_ids):
    rows, part = back.shape
    n = expert_ids.shape[0]
    return pl.pallas_call(
        collect_kernel,
        out_shape=jax.ShapeDtypeStruct((n, 8 * part), BF16),
        compiler_params=pltpu.CompilerParams(vmem_limit_bytes=8 << 20),
        name="collect",
        cost_estimate=pl.CostEstimate(flops=4 * 10**8, bytes_accessed=15 * 10**5, transcendentals=0),
    )(back, expert_ids)


def swap(x):
    return lax.ppermute(x, "core", [(0, 1), (1, 0)])


def turn(x, ring):
    pairs = [(2 * y + c, 2 * ((y + 1 - 2 * c) % ring) + c) for y in range(ring) for c in range(2)]
    return lax.ppermute(x, ("y", "core"), pairs)


def shards(tokens, scores, expert_ids, gate_halves, up_halves, shared_gate, shared_up):
    ring = lax.axis_size("y")
    chips = lax.axis_size("wide") * ring
    partner = swap(tokens)
    send = dispatch(tokens, scores, expert_ids, chips)
    send, partner = lax.optimization_barrier((send, partner))
    arrived = lax.all_to_all(
        send.reshape(chips, 8, send.shape[1]), ("wide", "y"), split_axis=0, concat_axis=0, tiled=True
    ).reshape(send.shape)
    gate = pltpu.with_memory_space_constraint(gate_halves[0], pltpu.VMEM)
    up = pltpu.with_memory_space_constraint(up_halves[0], pltpu.VMEM)
    arrived, mine = lax.optimization_barrier((arrived, tokens))
    arrived_other = swap(arrived)
    opposite = lax.ppermute(mine, "y", [(y, (y + ring // 2) % ring) for y in range(ring)])
    own_hidden, pair = routed_own(arrived, gate, up, mine, partner)
    turned = turn(pair, ring)
    hidden = routed_other(arrived_other, own_hidden, gate, up)
    back = lax.all_to_all(
        hidden.reshape(2 * chips, 8, hidden.shape[3]),
        ("wide", "y", "core"),
        split_axis=0,
        concat_axis=0,
        tiled=True,
    ).reshape(16 * chips, hidden.shape[3])
    turned, opposite, _ = lax.optimization_barrier((turned, opposite, hidden))
    blocks = (tokens, partner, turned, swap(turned), opposite, swap(opposite))
    shared_hidden = shared(blocks, shared_gate, shared_up, 2 * ring * tokens.shape[0])
    back, shared_hidden = lax.optimization_barrier((back, shared_hidden))
    return collect(back, expert_ids), shared_hidden


def solution(mesh):
    wide, narrow = mesh.devices.shape
    fine = Mesh(mesh.devices.reshape(wide, narrow // 2, 2), ("wide", "y", "core"))
    every = ("wide", "y", "core")
    placed = (
        P(every, None),
        P(every),
        P(every),
        P(every, None, None),
        P(every, None, None),
        P(None, ("y", "core")),
        P(None, ("y", "core")),
    )
    return jax.shard_map(
        shards,
        mesh=fine,
        in_specs=placed,
        out_specs=(P(every, None), P("wide", ("y", "core"))),
        check_vma=False,
    )
```
